32 devices in a mesh: gy: 8 (over y, x, core), gz: 4 (over z).
Axes of the slice: x: 2, y: 2, z: 4, core: 2. Of those that a mesh axis runs over, the one named last changes fastest.
Arguments:
- pressure_cotangent: bfloat16 [32, 1024, 2048], P('gz', 'gy'), may hold values from -6 to 6
- velocity_cotangent: bfloat16 [32, 1024, 2048], P('gz', 'gy'), may hold values from -6 to 6
- inverse_spacing: float32 [32], P('gz'), may hold values from 0.5 to 4
- inverse_pivot: float32 [32, 2048, 1024], P('gz', 'gy'), may hold values from 0.02 to 0.1
- lower_factor: float32 [32, 2048, 1024], P('gz', 'gy'), may hold values from 0.04 to 0.998, as said below
- upper_factor: float32 [32, 2048, 1024], P('gz', 'gy'), may hold values from 0.04 to 0.998, as said below
Outputs:
- pressure_adjoint: bfloat16 [32, 1024, 2048], P('gz', 'gy')
The draws below stay inside these ranges and needn't reach their ends.
Inputs may be any that keep to these rules, and one draw needn't show every extreme that they name: `lower_factor`: multiplier carried from one level to the next. `upper_factor`: multiplier carried from one level to the next.
All inputs are finite; a program needn't handle non-finite values.
Results may differ from the reference program's by a relative error of at most 0.0018.
Values may be sent and summed in bfloat16 or wider, within the bound.
A program may use at most 192 MiB of HBM per device.

```python
import math
import jax
import jax.numpy as jnp
from jax import lax

NX = 2048
NY = 1024
VERTICAL_LAYERS = 32


def rate_field(key):
    stochastic_seed_sequence = jax.random.split(key, 6)
    slow_share = 0.5
    slow_mask = jax.random.bernoulli(stochastic_seed_sequence[0], slow_share, (1, NX, NY))
    slow_rate = jax.random.uniform(stochastic_seed_sequence[1], (1, NX, NY), jnp.float32, 0.93, 0.998)
    fast_rate = jax.random.uniform(stochastic_seed_sequence[2], (1, NX, NY), jnp.float32, 0.1, 0.6)
    base_rate = jnp.where(slow_mask, slow_rate, fast_rate)
    jitter = jax.random.uniform(stochastic_seed_sequence[3], (VERTICAL_LAYERS, NX, NY), jnp.float32, 0.97, 1.0)
    sudden_level_set = jax.random.randint(stochastic_seed_sequence[4], (2,), 0, VERTICAL_LAYERS)
    level_heights = jnp.arange(VERTICAL_LAYERS)
    abrupt_change_indicator = jnp.any(level_heights[:, None] == sudden_level_set[None, :], axis=1)
    abrupt_change_cutoff = jax.random.uniform(stochastic_seed_sequence[5], (VERTICAL_LAYERS, 1, 1), jnp.float32, 0.5, 0.8)
    decomposition_coefficients = jnp.where(abrupt_change_indicator[:, None, None], abrupt_change_cutoff, 1.0)
    return (base_rate * jitter * decomposition_coefficients).astype(jnp.float32)


def draw_lower_factor(key, part):
    return rate_field(jax.random.fold_in(key, 11))


def draw_upper_factor(key, part):
    return rate_field(jax.random.fold_in(key, 23))


def level_of(key, extent, cuts, low, high):
    gain, own = 1.0, jax.random.fold_in(key, 6)
    for axis_at, parts in cuts:
        heights = jnp.exp(jax.random.uniform(jax.random.fold_in(own, axis_at), (parts,), jnp.float32, low / len(cuts), high / len(cuts)))
        gain = gain * jnp.repeat(heights, extent[axis_at] // parts).reshape([-1 if axis == axis_at else 1 for axis in range(len(extent))])
    return gain


def bell_draw(rng, extent, width, bound, shards=(), kind=jnp.bfloat16):
    level = level_of(rng, extent, shards, -0.22, 0.18) if shards else 1.0
    result = jax.random.normal(rng, extent, jnp.float32) * width * level
    return jnp.minimum(jnp.maximum(result, -bound), bound).astype(kind)


def setup_inputs(seed: int = 0) -> dict:
    key_of = jax.random.split(jax.random.key(seed), 7)
    return {
        "pressure_cotangent": bell_draw(key_of[0], (VERTICAL_LAYERS, NY, NX), 1.0, 6.0, ((0, 4), (1, 8))),
        "velocity_cotangent": bell_draw(key_of[1], (VERTICAL_LAYERS, NY, NX), 1.0, 6.0, ((0, 4), (1, 8))),
        "inverse_spacing": jnp.clip(jnp.exp(math.log(4.0) - 2.0794415 * jax.random.uniform(key_of[2], (VERTICAL_LAYERS,), jnp.float32) ** level_of(key_of[2], (VERTICAL_LAYERS,), ((0, 4),), -0.2, 0.2)), 0.5, 4.0),
        "inverse_pivot": jnp.clip(jnp.exp(math.log(0.1) - 1.609438 * jax.random.uniform(key_of[3], (VERTICAL_LAYERS, NX, NY), jnp.float32) ** level_of(key_of[3], (VERTICAL_LAYERS, NX, NY), ((0, 4), (1, 8)), -0.2, 0.2)), 0.02, 0.1),
        "lower_factor": draw_lower_factor(jax.random.fold_in(key_of[6], 71), 0),
        "upper_factor": draw_upper_factor(jax.random.fold_in(key_of[6], 71), 0),
    }


def reference(pressure_cotangent, velocity_cotangent, inverse_spacing, inverse_pivot, lower_factor, upper_factor):
    velocity = velocity_cotangent.astype(jnp.float32)
    shifted = jnp.concatenate([velocity[1:], jnp.zeros_like(velocity[:1])], 0)
    source = pressure_cotangent.astype(jnp.float32) + inverse_spacing[:, None, None] * (shifted - velocity)
    spectrum = jnp.fft.fft2(source, axes=(1, 2))
    spectrum = jnp.transpose(spectrum, (0, 2, 1))
    empty_field = jnp.zeros(spectrum.shape[1:], spectrum.dtype)

    def advance_down(running, layer_values):
        forcing, pivot_values, lower_values = layer_values
        running = pivot_values * forcing + lower_values * running
        return running, running

    _, lowered = lax.scan(advance_down, empty_field, (spectrum, inverse_pivot, lower_factor))

    def advance_up(running, layer_values):
        forcing, upper_values = layer_values
        running = forcing + upper_values * running
        return running, running

    _, solved = lax.scan(advance_up, empty_field, (lowered, upper_factor), reverse=True)
    pressure_field = jnp.fft.ifft2(jnp.transpose(solved, (0, 2, 1)), axes=(1, 2)).real
    return pressure_field.astype(jnp.bfloat16)
```

```python
import functools
import math

import jax
import jax.numpy as jnp
from jax import lax
from jax.experimental import pallas as pl
from jax.sharding import PartitionSpec as P

PREC = lax.Precision.HIGH
F32 = jnp.float32


def passed_along(x, axis, by):
    size = lax.axis_size(axis)
    pairs = [(i, i + by) for i in range(size) if 0 <= i + by < size]
    return lax.ppermute(x, axis, pairs)


def unit_circle(phase, count):
    angle = (phase % count).astype(F32) * (2.0 * math.pi / count)
    return jnp.cos(angle), jnp.sin(angle)


def circle_table(count):
    low = 32
    high = count // low
    k = jnp.arange(count, dtype=jnp.int32)[None, :]
    ch, sh = unit_circle(jnp.arange(high, dtype=jnp.int32)[:, None] * low * k, count)
    cl, sl = unit_circle(jnp.arange(low, dtype=jnp.int32)[:, None] * k, count)
    ch, sh, cl, sl = lax.optimization_barrier((ch, sh, cl, sl))
    ch, sh, cl, sl = ch[:, None], sh[:, None], cl[None], sl[None]
    cosine = (ch * cl - sh * sl).reshape(count, count)
    sine = (sh * cl + ch * sl).reshape(count, count)
    return cosine, sine


def split_table(count, half):
    low = 32
    column = jnp.arange(2 * count, dtype=jnp.int32)[None, :]
    k = column // (2 * half) * half + column % half
    quarter = jnp.where(column % (2 * half) < half, 0, count // 4)
    ch, sh = unit_circle(jnp.arange(count // low, dtype=jnp.int32)[:, None] * low * k, count)
    cl, sl = unit_circle(jnp.arange(low, dtype=jnp.int32)[:, None] * k + quarter, count)
    ch, sh, cl, sl = lax.optimization_barrier((ch, sh, cl, sl))
    return (ch[:, None] * cl[None] - sh[:, None] * sl[None]).reshape(count, 2 * count)


def down_kernel(chunks, per, *refs):
    cos_refs, sin_refs = refs[:chunks], refs[chunks : 2 * chunks]
    pivot, lower, low, summary = refs[2 * chunks :]
    re = im = jnp.zeros(pivot.shape[1:], F32)
    gain = jnp.ones(pivot.shape[1:], F32)
    for z in range(chunks * per):
        c, s = cos_refs[z // per], sin_refs[z // per]
        q = z % per
        d, m = pivot[z], lower[z]
        re = d * (c[q, 0] + s[q, 1]) + m * re
        im = d * (c[q, 1] - s[q, 0]) + m * im
        gain = m * gain
        low[z, 0] = re
        low[z, 1] = im
    summary[0] = gain
    summary[1] = re
    summary[2] = im


def up_summary_kernel(levels, low, lower, upper, enter, summary):
    er, ei = enter[0, 0], enter[0, 1]
    re = im = jnp.zeros(lower.shape[1:], F32)
    gain = jnp.ones(lower.shape[1:], F32)
    carried = jnp.ones(lower.shape[1:], F32)
    for z in range(levels):
        carried = carried * lower[z]
        re = re + gain * (low[z, 0] + carried * er)
        im = im + gain * (low[z, 1] + carried * ei)
        gain = gain * upper[z]
    summary[0] = gain
    summary[1] = re
    summary[2] = im


def solve_kernel(levels, per, low, lower, upper, enter, above, *outs):
    er, ei = enter[0, 0], enter[0, 1]
    gains = []
    carried = jnp.ones(lower.shape[1:], F32)
    for z in range(levels):
        carried = carried * lower[z]
        gains.append(carried)
    re, im = above[0, 0], above[0, 1]
    for z in range(levels - 1, -1, -1):
        re = low[z, 0] + gains[z] * er + upper[z] * re
        im = low[z, 1] + gains[z] * ei + upper[z] * im
        outs[z // per][z % per, 0] = re
        outs[z // per][z % per, 1] = im


def entering(summary, reverse):
    count = lax.axis_size("gz")
    _, width, span = summary.shape
    parts = summary.reshape(3, count, width // count, span)
    got = lax.all_to_all(parts, "gz", split_axis=1, concat_axis=1, tiled=True)
    order = list(range(count))
    if reverse:
        order.reverse()
    states = [None] * count
    state = jnp.zeros((2, width // count, span), F32)
    for at in order:
        states[at] = state
        state = got[1:, at] + got[0, at][None] * state
    return lax.all_to_all(jnp.stack(states), "gz", split_axis=0, concat_axis=0, tiled=True)


def on_device(
    pressure_cotangent,
    velocity_cotangent,
    inverse_spacing,
    inverse_pivot,
    lower_factor,
    upper_factor,
):
    levels, rows, nx = pressure_cotangent.shape
    level_above = passed_along(velocity_cotangent[:1], "gz", -1)
    gy = lax.axis_size("gy")
    gz = lax.axis_size("gz")
    ny = rows * gy
    half = nx // gy
    per = 2 if levels % 2 == 0 else 1
    chunks = levels // per
    velocity = velocity_cotangent.astype(F32)
    shifted = jnp.concatenate([velocity[1:], level_above.astype(F32)], 0)
    source = pressure_cotangent.astype(F32) + inverse_spacing[:, None, None] * (shifted - velocity)

    table = lax.optimization_barrier(split_table(nx, half))
    cy, sy = lax.optimization_barrier(circle_table(ny))

    cos_parts, sin_parts = [], []
    for i in range(chunks):
        piece = source[i * per : (i + 1) * per]
        spec = jnp.einsum("zyn,nc->zyc", piece, table, precision=PREC)
        spec = jnp.transpose(spec.reshape(per, rows, gy, 2 * half), (2, 0, 1, 3))
        got = lax.all_to_all(spec, "gy", split_axis=0, concat_axis=0, tiled=True)
        got = jnp.transpose(got, (1, 0, 2, 3)).reshape(per, ny, 2 * half)
        c = jnp.einsum("zyc,yk->zck", got, cy, precision=PREC)
        s = jnp.einsum("zyc,yk->zck", got, sy, precision=PREC)
        cos_parts.append(c.reshape(per, 2, half, ny))
        sin_parts.append(s.reshape(per, 2, half, ny))

    quarter = half // gz
    kb = min(16, quarter)
    in_quarter = quarter // kb
    grid = (half // kb,)
    chunk_spec = pl.BlockSpec((per, 2, kb, ny), lambda i: (0, 0, i, 0))
    factor_spec = pl.BlockSpec((levels, kb, ny), lambda i: (0, i, 0))
    low_spec = pl.BlockSpec((levels, 2, kb, ny), lambda i: (0, 0, i, 0))
    summary_spec = pl.BlockSpec((3, kb, ny), lambda i: (0, i, 0))
    state_spec = pl.BlockSpec((1, 2, kb, ny), lambda i: (i // in_quarter, 0, i % in_quarter, 0))
    summary_shape = jax.ShapeDtypeStruct((3, half, ny), F32)

    low, summary = pl.pallas_call(
        functools.partial(down_kernel, chunks, per),
        grid=grid,
        in_specs=[chunk_spec] * (2 * chunks) + [factor_spec] * 2,
        out_specs=[low_spec, summary_spec],
        out_shape=[jax.ShapeDtypeStruct((levels, 2, half, ny), F32), summary_shape],
    )(*cos_parts, *sin_parts, inverse_pivot, lower_factor)
    enter = entering(summary, False)
    summary = pl.pallas_call(
        functools.partial(up_summary_kernel, levels),
        grid=grid,
        in_specs=[low_spec, factor_spec, factor_spec, state_spec],
        out_specs=summary_spec,
        out_shape=summary_shape,
    )(low, lower_factor, upper_factor, enter)
    above = entering(summary, True)
    solved = pl.pallas_call(
        functools.partial(solve_kernel, levels, per),
        grid=grid,
        in_specs=[low_spec, factor_spec, factor_spec, state_spec, state_spec],
        out_specs=[chunk_spec] * chunks,
        out_shape=[jax.ShapeDtypeStruct((per, 2, half, ny), F32)] * chunks,
    )(low, lower_factor, upper_factor, enter, above)

    normalizer = 1.0 / (nx * ny)
    fields = []
    for i in range(chunks):
        flat = solved[i].reshape(per, 2 * half, ny)
        c = jnp.einsum("ky,zck->zyc", cy, flat, precision=PREC)
        s = jnp.einsum("ky,zck->zyc", sy, flat, precision=PREC)
        back = jnp.concatenate([c[..., :half] - s[..., half:], c[..., half:] + s[..., :half]], 2)
        back = jnp.transpose(back.reshape(per, gy, rows, 2 * half), (1, 0, 2, 3))
        got = lax.all_to_all(back, "gy", split_axis=0, concat_axis=0, tiled=True)
        got = jnp.transpose(got, (1, 2, 0, 3)).reshape(per, rows, 2 * nx)
        field = jnp.einsum("zyc,nc->zyn", got, table, precision=PREC) * normalizer
        fields.append(field.astype(jnp.bfloat16))
    return jnp.concatenate(fields, 0)


def solution(mesh):
    spec = P("gz", "gy", None)
    return jax.shard_map(
        on_device,
        mesh=mesh,
        in_specs=(spec, spec, P("gz"), spec, spec, spec),
        out_specs=spec,
        check_vma=False,
    )
```

```python
import functools
import math

import jax
import jax.numpy as jnp
from jax import lax
from jax.experimental import pallas as pl
from jax.sharding import PartitionSpec as P

PREC = lax.Precision.HIGH
F32 = jnp.float32


def passed_along(x, axis, by):
    size = lax.axis_size(axis)
    pairs = [(i, i + by) for i in range(size) if 0 <= i + by < size]
    return lax.ppermute(x, axis, pairs)


def unit_circle(phase, count):
    angle = (phase % count).astype(F32) * (2.0 * math.pi / count)
    return jnp.cos(angle), jnp.sin(angle)


def circle_table(count):
    low = 32
    high = count // low
    k = jnp.arange(count, dtype=jnp.int32)[None, :]
    ch, sh = unit_circle(jnp.arange(high, dtype=jnp.int32)[:, None] * low * k, count)
    cl, sl = unit_circle(jnp.arange(low, dtype=jnp.int32)[:, None] * k, count)
    ch, sh, cl, sl = lax.optimization_barrier((ch, sh, cl, sl))
    ch, sh, cl, sl = ch[:, None], sh[:, None], cl[None], sl[None]
    cosine = (ch * cl - sh * sl).reshape(count, count)
    sine = (sh * cl + ch * sl).reshape(count, count)
    return cosine, sine


def split_table(count, half):
    low = 32
    column = jnp.arange(2 * count, dtype=jnp.int32)[None, :]
    k = column // (2 * half) * half + column % half
    quarter = jnp.where(column % (2 * half) < half, 0, count // 4)
    ch, sh = unit_circle(jnp.arange(count // low, dtype=jnp.int32)[:, None] * low * k, count)
    cl, sl = unit_circle(jnp.arange(low, dtype=jnp.int32)[:, None] * k + quarter, count)
    ch, sh, cl, sl = lax.optimization_barrier((ch, sh, cl, sl))
    return (ch[:, None] * cl[None] - sh[:, None] * sl[None]).reshape(count, 2 * count)


def down_kernel(chunks, per, *refs):
    cos_refs, sin_refs = refs[:chunks], refs[chunks : 2 * chunks]
    pivot, lower, low, summary = refs[2 * chunks :]
    re = im = jnp.zeros(pivot.shape[1:], F32)
    gain = jnp.ones(pivot.shape[1:], F32)
    for z in range(chunks * per):
        c, s = cos_refs[z // per], sin_refs[z // per]
        q = z % per
        d, m = pivot[z], lower[z]
        re = d * (c[q, 0] + s[q, 1]) + m * re
        im = d * (c[q, 1] - s[q, 0]) + m * im
        gain = m * gain
        low[z, 0] = re
        low[z, 1] = im
    summary[0] = gain
    summary[1] = re
    summary[2] = im


def up_summary_kernel(levels, low, lower, upper, enter, summary):
    er, ei = enter[0, 0], enter[0, 1]
    re = im = jnp.zeros(lower.shape[1:], F32)
    gain = jnp.ones(lower.shape[1:], F32)
    carried = jnp.ones(lower.shape[1:], F32)
    for z in range(levels):
        carried = carried * lower[z]
        re = re + gain * (low[z, 0] + carried * er)
        im = im + gain * (low[z, 1] + carried * ei)
        gain = gain * upper[z]
    summary[0] = gain
    summary[1] = re
    summary[2] = im


def solve_kernel(levels, per, low, lower, upper, enter, above, *outs):
    er, ei = enter[0, 0], enter[0, 1]
    gains = []
    carried = jnp.ones(lower.shape[1:], F32)
    for z in range(levels):
        carried = carried * lower[z]
        gains.append(carried)
    re, im = above[0, 0], above[0, 1]
    for z in range(levels - 1, -1, -1):
        re = low[z, 0] + gains[z] * er + upper[z] * re
        im = low[z, 1] + gains[z] * ei + upper[z] * im
        outs[z // per][z % per, 0] = re
        outs[z // per][z % per, 1] = im


def entering(summary, reverse):
    count = lax.axis_size("gz")
    _, width, span = summary.shape
    parts = summary.reshape(3, count, width // count, span)
    got = lax.all_to_all(parts, "gz", split_axis=1, concat_axis=1, tiled=True)
    order = list(range(count))
    if reverse:
        order.reverse()
    states = [None] * count
    state = jnp.zeros((2, width // count, span), F32)
    for at in order:
        states[at] = state
        state = got[1:, at] + got[0, at][None] * state
    return lax.all_to_all(jnp.stack(states), "gz", split_axis=0, concat_axis=0, tiled=True)


def on_device(
    pressure_cotangent,
    velocity_cotangent,
    inverse_spacing,
    inverse_pivot,
    lower_factor,
    upper_factor,
):
    levels, rows, nx = pressure_cotangent.shape
    level_above = passed_along(velocity_cotangent[:1], "gz", -1)
    gy = lax.axis_size("gy")
    gz = lax.axis_size("gz")
    ny = rows * gy
    half = nx // gy
    per = 2 if levels % 2 == 0 else 1
    chunks = levels // per
    velocity = velocity_cotangent.astype(F32)
    shifted = jnp.concatenate([velocity[1:], level_above.astype(F32)], 0)
    source = pressure_cotangent.astype(F32) + inverse_spacing[:, None, None] * (shifted - velocity)

    table = lax.optimization_barrier(split_table(nx, half))
    cy, sy = lax.optimization_barrier(circle_table(ny))

    cos_parts, sin_parts = [], []
    for i in range(chunks):
        piece = source[i * per : (i + 1) * per]
        spec = jnp.einsum("zyn,nc->zyc", piece, table, precision=PREC)
        spec = jnp.transpose(spec.reshape(per, rows, gy, 2 * half), (2, 0, 1, 3))
        if i >= 2:
            spec, cos_parts[i - 2], sin_parts[i - 2] = lax.optimization_barrier(
                (spec, cos_parts[i - 2], sin_parts[i - 2])
            )
        got = lax.all_to_all(spec, "gy", split_axis=0, concat_axis=0, tiled=True)
        got = jnp.transpose(got, (1, 0, 2, 3)).reshape(per, ny, 2 * half)
        c = jnp.einsum("zyc,yk->zck", got, cy, precision=PREC)
        s = jnp.einsum("zyc,yk->zck", got, sy, precision=PREC)
        cos_parts.append(c.reshape(per, 2, half, ny))
        sin_parts.append(s.reshape(per, 2, half, ny))

    quarter = half // gz
    kb = min(16, quarter)
    in_quarter = quarter // kb
    grid = (half // kb,)
    chunk_spec = pl.BlockSpec((per, 2, kb, ny), lambda i: (0, 0, i, 0))
    factor_spec = pl.BlockSpec((levels, kb, ny), lambda i: (0, i, 0))
    low_spec = pl.BlockSpec((levels, 2, kb, ny), lambda i: (0, 0, i, 0))
    summary_spec = pl.BlockSpec((3, kb, ny), lambda i: (0, i, 0))
    state_spec = pl.BlockSpec((1, 2, kb, ny), lambda i: (i // in_quarter, 0, i % in_quarter, 0))
    summary_shape = jax.ShapeDtypeStruct((3, half, ny), F32)

    low, summary = pl.pallas_call(
        functools.partial(down_kernel, chunks, per),
        grid=grid,
        in_specs=[chunk_spec] * (2 * chunks) + [factor_spec] * 2,
        out_specs=[low_spec, summary_spec],
        out_shape=[jax.ShapeDtypeStruct((levels, 2, half, ny), F32), summary_shape],
    )(*cos_parts, *sin_parts, inverse_pivot, lower_factor)
    enter = entering(summary, False)
    summary = pl.pallas_call(
        functools.partial(up_summary_kernel, levels),
        grid=grid,
        in_specs=[low_spec, factor_spec, factor_spec, state_spec],
        out_specs=summary_spec,
        out_shape=summary_shape,
    )(low, lower_factor, upper_factor, enter)
    above = entering(summary, True)
    solved = pl.pallas_call(
        functools.partial(solve_kernel, levels, per),
        grid=grid,
        in_specs=[low_spec, factor_spec, factor_spec, state_spec, state_spec],
        out_specs=[chunk_spec] * chunks,
        out_shape=[jax.ShapeDtypeStruct((per, 2, half, ny), F32)] * chunks,
    )(low, lower_factor, upper_factor, enter, above)

    normalizer = 1.0 / (nx * ny)
    fields = []
    for i in range(chunks):
        flat = solved[i].reshape(per, 2 * half, ny)
        c = jnp.einsum("ky,zck->zyc", cy, flat, precision=PREC)
        s = jnp.einsum("ky,zck->zyc", sy, flat, precision=PREC)
        back = jnp.concatenate([c[..., :half] - s[..., half:], c[..., half:] + s[..., :half]], 2)
        back = jnp.transpose(back.reshape(per, gy, rows, 2 * half), (1, 0, 2, 3))
        if i >= 2:
            back, fields[i - 2] = lax.optimization_barrier((back, fields[i - 2]))
        got = lax.all_to_all(back, "gy", split_axis=0, concat_axis=0, tiled=True)
        got = jnp.transpose(got, (1, 2, 0, 3)).reshape(per, rows, 2 * nx)
        field = jnp.einsum("zyc,nc->zyn", got, table, precision=PREC) * normalizer
        fields.append(field.astype(jnp.bfloat16))
    return jnp.concatenate(fields, 0)


def solution(mesh):
    spec = P("gz", "gy", None)
    return jax.shard_map(
        on_device,
        mesh=mesh,
        in_specs=(spec, spec, P("gz"), spec, spec, spec),
        out_specs=spec,
        check_vma=False,
    )
```
